32 devices in a mesh: row: 8 (over y, x, core), col: 4 (over z).
Axes of the slice: x: 2, y: 2, z: 4, core: 2. Of those that a mesh axis runs over, the one named last changes fastest.
Arguments:
- sub_basis: bfloat16 [32, 768, 768], P(('row', 'col')), may hold values from -0.15625 to 0.15625
- coupling: bfloat16 [32, 2, 768, 768], P(('row', 'col')), may hold values from -0.15625 to 0.15625
- pair_live: int32 [32, 2], P(('row', 'col')), may hold values 0 or 1
- offsets: int32 [32], P(('row', 'col')), may hold values from 0 to 3328
- dual_in: float32 [4, 4096], P('col', 'row'), may hold values from -6 to 6
Outputs:
- dual_out: float32 [4, 4096], P('col', 'row')
The draws below stay inside these ranges and needn't reach their ends.
Inputs may be any that keep to these rules, and one draw needn't show every extreme that they name: `offsets`: each subdomain's window of 768 multipliers lies inside its block column's vector.
All inputs are finite; a program needn't handle non-finite values. No bound on the sum of `pair_live` on one device may be relied on, other than what follows from the above.
Results may differ from the reference program's by a relative error of at most 0.0085.
Values may be sent and summed in bfloat16 or wider, within the bound.
A program may use at most 64 MiB of HBM per device.

```python
import jax
import jax.numpy as jnp
from jax import lax

W = 768
K = 768
HOPS = 2
SLICE = 512
SUBS = 32
DUALS = 4096
N_ROW = 8
N_COL = 4


def place_ends(array, key, least, high):
    longest = array.shape.index(max(array.shape))
    spots = []
    for shift in (0, 1):
        where = [jax.random.randint(jax.random.fold_in(key, axis), (), 0, length) for axis, length in enumerate(array.shape)]
        where[longest] = (where[longest] + shift) % array.shape[longest]
        spots.append(tuple(where))
    return array.at[spots[0]].set(least).at[spots[1]].set(high)


def shard_levels(own_key, dims, split, smallest, top_value):
    loudness = 1.0
    for position, shards_of in split:
        draws = jax.random.uniform(jax.random.fold_in(jax.random.fold_in(own_key, 6), position), (shards_of,), jnp.float32, smallest / len(split), top_value / len(split))
        loudness = loudness * jnp.repeat(jnp.exp(draws), dims[position] // shards_of).reshape((-1,) + (1,) * (len(dims) - 1 - position))
    return loudness


def scatter_about(key, dims, spread, reach, shards=(), kind=jnp.bfloat16):
    array = jax.random.normal(key, dims, jnp.float32) * spread
    if len(shards) > 0:
        array = shard_levels(key, dims, shards, -0.22, 0.18) * array
    return jnp.clip(array, min=-reach, max=reach).astype(kind)


def setup_inputs(seed: int = 0) -> dict:
    key_list = jax.random.split(jax.random.key(seed), 6)
    return {
        "sub_basis": scatter_about(key_list[0], (SUBS, K, W), (2 * K) ** -0.5, 0.15625, ((0, 32),)),
        "coupling": scatter_about(key_list[1], (SUBS, HOPS, K, W), (2 * K) ** -0.5, 0.15625, ((0, 32),)),
        "pair_live": place_ends((jax.random.randint(key_list[2], (SUBS, HOPS), 0, 4) < 3).astype(jnp.int32), jax.random.fold_in(key_list[2], 1), 0, 1),
        "offsets": place_ends(jax.random.randint(key_list[3], (SUBS,), 0, DUALS - W + 1), jax.random.fold_in(key_list[3], 1), 0, DUALS - W).astype(jnp.int32),
        "dual_in": scatter_about(key_list[4], (N_COL, DUALS), 1.0, 6.0, ((0, 4), (1, 8)), jnp.float32),
    }


def form_blocks(sub_basis, coupling, pair_live):
    def single(items):
        basis_one, coupling_one, live_one = items
        made = jnp.einsum("kv,hkw->hvw", basis_one.astype(jnp.float32), coupling_one.astype(jnp.float32), precision=lax.Precision.HIGHEST)
        made = made.astype(jnp.bfloat16)
        return made * live_one[:, None, None].astype(jnp.bfloat16)
    return lax.map(single, (sub_basis, coupling, pair_live))


def apply_dual(column_vec, sub_basis, blocks, offsets):
    count = sub_basis.shape[0]
    columns = (jnp.arange(count, dtype=jnp.int32) % N_COL).astype(jnp.int32)

    def cut_window(column, first_index):
        return lax.dynamic_slice(column_vec, (column.astype(jnp.int32), first_index.astype(jnp.int32)), (1, W))[0]

    windows = jax.vmap(cut_window)(columns, offsets)
    grid = windows.reshape(N_ROW, N_COL, W)
    leading = jnp.stack([jnp.roll(grid, -(slot_index + 1), axis=1).reshape(count, W) for slot_index in range(HOPS)], axis=1)

    def single(items):
        basis_one, blocks_one, window, leading_one = items
        projected = jnp.dot(basis_one, window, precision=lax.Precision.HIGHEST)
        summed = jnp.dot(projected, basis_one, precision=lax.Precision.HIGHEST)
        widened = blocks_one.astype(jnp.float32)
        summed = summed + jnp.einsum("hvw,hw->v", widened, leading_one, precision=lax.Precision.HIGHEST)
        backward = jnp.einsum("hvw,v->hw", widened, window, precision=lax.Precision.HIGHEST)
        return summed, backward

    totals, backs = lax.map(single, (sub_basis, blocks, windows, leading))
    backs = backs.reshape(N_ROW, N_COL, HOPS, W)
    for slot_index in range(HOPS):
        totals = totals + jnp.roll(backs[:, :, slot_index], slot_index + 1, axis=1).reshape(count, W)
    positions = offsets[:, None].astype(jnp.int32) + jnp.arange(W, dtype=jnp.int32)[None, :]
    result = jnp.zeros((N_COL, N_ROW * SLICE), jnp.float32)
    return result.at[columns[:, None], positions].add(totals)


def reference(sub_basis, coupling, pair_live, offsets, dual_in):
    blocks = form_blocks(sub_basis, coupling, pair_live)
    first_product = apply_dual(dual_in, sub_basis, blocks, offsets)
    return apply_dual(first_product, sub_basis, blocks, offsets)
```

```python
import jax
import jax.numpy as jnp
from jax import lax
from jax.sharding import PartitionSpec as P


def passed_along(array, axis, by):
    count = lax.axis_size(axis)
    return lax.ppermute(array, axis, [(i, (i + by) % count) for i in range(count)])


def left_apply(matrix, vector):
    return lax.dot_general(
        matrix, vector, (((1,), (0,)), ((), ())),
        precision=lax.Precision.HIGHEST, preferred_element_type=jnp.float32,
    )


def right_apply(vector, matrix):
    return jnp.dot(vector, matrix, precision=lax.Precision.HIGHEST, preferred_element_type=jnp.float32)


def apply_dual(window, basis, couplings, live):
    projected = left_apply(basis, window)
    inner = projected
    summed = jnp.zeros_like(window)
    for slot, coupling in enumerate(couplings):
        distance = slot + 1
        ahead = passed_along(window, "col", -distance)
        inner = inner + live[slot] * left_apply(coupling, ahead)
        back = live[slot] * right_apply(projected, coupling)
        summed = summed + passed_along(back, "col", distance)
    return summed + right_apply(inner, basis)


def on_device(sub_basis, coupling, pair_live, offsets, dual_in):
    width = sub_basis.shape[2]
    basis = sub_basis[0].astype(jnp.float32)
    couplings = [coupling[0, h].astype(jnp.float32) for h in range(coupling.shape[1])]
    live = pair_live[0].astype(jnp.float32)
    length = dual_in.shape[1] * lax.axis_size("row")
    start = offsets[0]
    piece = dual_in
    for _ in range(2):
        column = lax.all_gather(piece, "row", axis=1, tiled=True)[0]
        window = lax.dynamic_slice_in_dim(column, start, width)
        local = apply_dual(window, basis, couplings, live)
        placed = lax.dynamic_update_slice(jnp.zeros((length,), jnp.float32), local, (start,))
        piece = lax.psum_scatter(placed[None, :], "row", scatter_dimension=1, tiled=True)
    return piece


def solution(mesh):
    return jax.shard_map(
        on_device,
        mesh=mesh,
        in_specs=(
            P(("row", "col"), None, None),
            P(("row", "col"), None, None, None),
            P(("row", "col"), None),
            P(("row", "col")),
            P("col", "row"),
        ),
        out_specs=P("col", "row"),
        check_vma=False,
    )
```

```python
import jax
import jax.numpy as jnp
from jax import lax
from jax.experimental import pallas as pl
from jax.experimental.pallas import tpu as pltpu
from jax.sharding import PartitionSpec as P

LANES = 128
MESH = pl.DeviceIdType.MESH


def split_rows(vector):
    high = vector.astype(jnp.bfloat16).astype(jnp.float32)
    rest = vector - high
    middle = rest.astype(jnp.bfloat16).astype(jnp.float32)
    lowest = rest - middle
    row = lax.broadcasted_iota(jnp.int32, vector.shape, 0)
    picked = jnp.where(row == 0, high, jnp.where(row == 1, middle, lowest))
    return jnp.where(row < 3, picked, 0.0).astype(jnp.bfloat16)


def spread(products):
    return jnp.broadcast_to(jnp.sum(products, axis=0, keepdims=True), products.shape)


def left_apply(matrix, vector):
    return spread(lax.dot_general(
        split_rows(vector), matrix, (((1,), (1,)), ((), ())),
        preferred_element_type=jnp.float32,
    ))


def right_apply(rows, matrix):
    return spread(jnp.dot(rows, matrix, preferred_element_type=jnp.float32))


def kernel(n_row, n_col, hops, basis_hbm, coupling_hbm, live_ref, offset_ref, dual_ref, out_ref,
           mats, gathered, column, placing, outgoing, incoming, sums, far_offsets,
           load_sems, send_sems, recv_sems, offset_send, offset_recv):
    me_row, me_col = lax.axis_index("row"), lax.axis_index("col")
    sides = hops + 1
    part_rows = dual_ref.shape[0]
    rows = n_row * part_rows
    width = mats.shape[2]
    chunks = width // LANES
    others = sides * n_row - 1

    loads = [pltpu.make_async_copy(basis_hbm.at[0], mats.at[0], load_sems.at[0])]
    for h in range(hops):
        loads.append(pltpu.make_async_copy(coupling_hbm.at[0, h], mats.at[h + 1], load_sems.at[h + 1]))
    for load in loads:
        load.start()

    barrier = pltpu.get_barrier_semaphore()
    shifts = sorted({d % n_col for d in range(-hops, hops + 1)})
    for shift in shifts:
        col = lax.rem(me_col + shift, n_col)

        def greet(i, carry, col=col):
            pl.semaphore_signal(barrier, inc=1, device_id=(lax.rem(me_row + i, n_row), col), device_id_type=MESH)
            return carry

        lax.fori_loop(1 if shift == 0 else 0, n_row, greet, 0, unroll=True)

    for k in range(sides):
        column[k, rows:, :] = jnp.zeros((column.shape[1] - rows, LANES), jnp.float32)
        placing[k, :, :] = jnp.zeros(placing.shape[1:], jnp.float32)
    pl.semaphore_wait(barrier, len(shifts) * n_row - 1)

    offset_copies = []
    for h in range(hops):
        copy = pltpu.make_async_remote_copy(
            src_ref=offset_ref, dst_ref=far_offsets.at[h],
            send_sem=offset_send.at[h], recv_sem=offset_recv.at[h],
            device_id=(me_row, lax.rem(me_col + n_col - (h + 1), n_col)), device_id_type=MESH)
        copy.start()
        offset_copies.append(copy)

    lane = lax.broadcasted_iota(jnp.int32, (8, LANES), 1)
    sub = lax.broadcasted_iota(jnp.int32, (8, LANES), 0)

    def gather_start(app, source):
        for k in range(sides):
            col = lax.rem(me_col + n_col - k, n_col)

            def send(i, carry, k=k, col=col):
                pltpu.make_async_remote_copy(
                    src_ref=source, dst_ref=gathered.at[app, k * n_row + me_row],
                    send_sem=send_sems.at[2 * app], recv_sem=recv_sems.at[2 * app],
                    device_id=(lax.rem(me_row + i, n_row), col), device_id_type=MESH).start()
                return carry

            lax.fori_loop(1 if k == 0 else 0, n_row, send, 0, unroll=True)
        gathered[app, me_row] = source[...]

    def wait_all(ref, sem):
        pltpu.make_async_copy(ref.at[pl.ds(0, others)], ref.at[pl.ds(0, others)], sem).wait()

    def window(k, start):
        first = start // LANES
        within = start - first * LANES
        tile = column[k, pl.ds(first, 8), :]
        turned = pltpu.roll(tile, lax.rem(LANES - within, LANES), 1)
        after = pltpu.roll(turned, 7, 0)
        cut = jnp.where(lane < LANES - within, turned, after)
        return jnp.concatenate(
            [jnp.broadcast_to(cut[j:j + 1, :], (8, LANES)) for j in range(chunks)], axis=1)

    def place(k, start, vector):
        first = start // LANES
        within = start - first * LANES
        tile = jnp.zeros((8, LANES), jnp.float32)
        for j in range(chunks):
            tile = jnp.where(sub == j, vector[:, j * LANES:(j + 1) * LANES], tile)
        turned = pltpu.roll(tile, within, 1)
        before = pltpu.roll(turned, 1, 0)
        placing[k, rows:rows + 8, :] = jnp.where(lane >= within, turned, before)
        return first

    starts = None
    lives = [live_ref[0, h].astype(jnp.float32) for h in range(hops)]
    source = dual_ref
    for app in range(2):
        gather_start(app, source)
        if app == 0:
            for copy in offset_copies:
                copy.wait()
            starts = [offset_ref[0]] + [far_offsets[h, 0] for h in range(hops)]
        wait_all(gathered.at[app], recv_sems.at[2 * app])
        for k in range(sides):
            for r in range(n_row):
                column[k, r * part_rows:(r + 1) * part_rows, :] = gathered[app, k * n_row + r]
        windows = [window(k, starts[k]) for k in range(sides)]
        if app == 0:
            for load in loads:
                load.wait()
        projected = left_apply(mats[0], windows[0])
        inner = projected
        for h in range(hops):
            inner = inner + lives[h] * left_apply(mats[h + 1], windows[h + 1])
        seen = split_rows(projected)
        totals = [lives[h] * right_apply(seen, mats[h + 1]) for h in range(hops)]
        totals = [right_apply(split_rows(inner), mats[0])] + totals
        for k in range(sides):
            first = place(k, starts[k], totals[k])
            col = lax.rem(me_col + k, n_col)
            for t in range(n_row):
                outgoing[app, k * n_row + t] = placing[k, pl.ds(rows - first + t * part_rows, part_rows), :]

            def send(i, carry, k=k, col=col):
                row = lax.rem(me_row + i, n_row)
                pltpu.make_async_remote_copy(
                    src_ref=outgoing.at[app, k * n_row + row], dst_ref=incoming.at[app, k * n_row + me_row],
                    send_sem=send_sems.at[2 * app + 1], recv_sem=recv_sems.at[2 * app + 1],
                    device_id=(row, col), device_id_type=MESH).start()
                return carry

            lax.fori_loop(1 if k == 0 else 0, n_row, send, 0, unroll=True)
        incoming[app, me_row] = outgoing[app, me_row]
        wait_all(incoming.at[app], recv_sems.at[2 * app + 1])
        summed = jnp.sum(incoming[app], axis=0)
        if app == 0:
            sums[...] = summed
            source = sums
        else:
            out_ref[...] = summed
    for app in range(2):
        wait_all(gathered.at[app], send_sems.at[2 * app])
        wait_all(outgoing.at[app], send_sems.at[2 * app + 1])


def on_device(sub_basis, coupling, pair_live, offsets, dual_in):
    n_row, n_col = lax.axis_size("row"), lax.axis_size("col")
    hops = coupling.shape[1]
    sides = hops + 1
    size = dual_in.shape[1]
    part_rows = size // LANES
    rows = n_row * part_rows
    depth, width = sub_basis.shape[1:]
    smem = pl.BlockSpec(memory_space=pltpu.SMEM)
    vmem = pl.BlockSpec(memory_space=pltpu.VMEM)
    hbm = pl.BlockSpec(memory_space=pl.ANY)
    out = pl.pallas_call(
        lambda *refs: kernel(n_row, n_col, hops, *refs),
        out_shape=jax.ShapeDtypeStruct((part_rows, LANES), jnp.float32),
        in_specs=[hbm, hbm, smem, smem, vmem],
        out_specs=vmem,
        scratch_shapes=[
            pltpu.VMEM((sides, depth, width), jnp.bfloat16),
            pltpu.VMEM((2, sides * n_row, part_rows, LANES), jnp.float32),
            pltpu.VMEM((sides, rows + 8, LANES), jnp.float32),
            pltpu.VMEM((sides, 2 * rows + 8, LANES), jnp.float32),
            pltpu.VMEM((2, sides * n_row, part_rows, LANES), jnp.float32),
            pltpu.VMEM((2, sides * n_row, part_rows, LANES), jnp.float32),
            pltpu.VMEM((part_rows, LANES), jnp.float32),
            pltpu.SMEM((hops, 1), jnp.int32),
            pltpu.SemaphoreType.DMA((sides,)),
            pltpu.SemaphoreType.DMA((4,)),
            pltpu.SemaphoreType.DMA((4,)),
            pltpu.SemaphoreType.DMA((hops,)),
            pltpu.SemaphoreType.DMA((hops,)),
        ],
        compiler_params=pltpu.CompilerParams(
            collective_id=0, has_side_effects=True, vmem_limit_bytes=32 * 1024 * 1024),
    )(sub_basis, coupling, pair_live, offsets, dual_in.reshape(part_rows, LANES))
    return out.reshape(1, size)


def solution(mesh):
    return jax.shard_map(
        on_device,
        mesh=mesh,
        in_specs=(
            P(("row", "col"), None, None),
            P(("row", "col"), None, None, None),
            P(("row", "col"), None),
            P(("row", "col")),
            P("col", "row"),
        ),
        out_specs=P("col", "row"),
        check_vma=False,
    )
```

```python
import jax
import jax.numpy as jnp
from jax import lax
from jax.experimental import pallas as pl
from jax.experimental.pallas import tpu as pltpu
from jax.sharding import PartitionSpec as P

LANES = 128
MESH = pl.DeviceIdType.MESH


def split_rows(vector):
    high = vector.astype(jnp.bfloat16).astype(jnp.float32)
    rest = vector - high
    middle = rest.astype(jnp.bfloat16).astype(jnp.float32)
    lowest = rest - middle
    row = lax.broadcasted_iota(jnp.int32, vector.shape, 0)
    picked = jnp.where(row == 0, high, jnp.where(row == 1, middle, lowest))
    return jnp.where(row < 3, picked, 0.0).astype(jnp.bfloat16)


def spread(products):
    return jnp.broadcast_to(jnp.sum(products, axis=0, keepdims=True), products.shape)


def left_apply(matrix, vector):
    return spread(lax.dot_general(
        split_rows(vector), matrix, (((1,), (1,)), ((), ())),
        preferred_element_type=jnp.float32,
    ))


def right_apply(rows, matrix):
    return spread(jnp.dot(rows, matrix, preferred_element_type=jnp.float32))


def to_lanes(tile, chunks):
    return jnp.concatenate(
        [jnp.broadcast_to(tile[j:j + 1, :], (8, LANES)) for j in range(chunks)], axis=1)


def to_tile(vector, chunks):
    row = lax.broadcasted_iota(jnp.int32, (8, LANES), 0)
    tile = jnp.zeros((8, LANES), jnp.float32)
    for j in range(chunks):
        tile = jnp.where(row == j, vector[:, j * LANES:(j + 1) * LANES], tile)
    return tile


def kernel(n_row, n_col, hops, basis_hbm, coupling_hbm, live_hbm, offset_hbm, dual_hbm, out_ref,
           mats, gathered, column, cut_window, far_window, back_out, back_in, placing, outgoing, incoming,
           live_ref, offset_ref, load_sems, small_sems, gather_send, gather_recv,
           window_send, window_recv, back_send, back_recv, scatter_send, scatter_recv):
    me_row, me_col = lax.axis_index("row"), lax.axis_index("col")
    part_rows = dual_hbm.shape[0]
    rows = n_row * part_rows
    chunks = mats.shape[2] // LANES
    others = n_row - 1

    small = [
        pltpu.make_async_copy(dual_hbm, gathered.at[0, me_row], small_sems.at[0]),
        pltpu.make_async_copy(offset_hbm, offset_ref, small_sems.at[1]),
        pltpu.make_async_copy(live_hbm, live_ref, small_sems.at[2]),
    ]
    loads = [pltpu.make_async_copy(basis_hbm.at[0], mats.at[0], load_sems.at[0])]
    for h in range(hops):
        loads.append(pltpu.make_async_copy(coupling_hbm.at[0, h], mats.at[h + 1], load_sems.at[h + 1]))
    for copy in small + loads:
        copy.start()

    barrier = pltpu.get_barrier_semaphore()
    for i in range(1, n_row):
        pl.semaphore_signal(barrier, inc=1, device_id=(lax.rem(me_row + i, n_row), me_col), device_id_type=MESH)
    shifts = sorted({d % n_col for d in range(-hops, hops + 1)} - {0})
    for shift in shifts:
        pl.semaphore_signal(barrier, inc=1, device_id=(me_row, lax.rem(me_col + shift, n_col)), device_id_type=MESH)

    column[rows:, :] = jnp.zeros((column.shape[0] - rows, LANES), jnp.float32)
    placing[...] = jnp.zeros(placing.shape, jnp.float32)
    for copy in small:
        copy.wait()
    start = offset_ref[0]
    first = start // LANES
    within = start - first * LANES
    lives = [live_ref[0, h].astype(jnp.float32) for h in range(hops)]
    lane = lax.broadcasted_iota(jnp.int32, (8, LANES), 1)
    pl.semaphore_wait(barrier, others + len(shifts))

    def row_peer(i):
        return lax.rem(me_row + i, n_row)

    def col_peer(shift):
        return (me_row, lax.rem(me_col + (shift % n_col), n_col))

    def wait_others(ref, sem):
        pltpu.make_async_copy(ref.at[pl.ds(0, others)], ref.at[pl.ds(0, others)], sem).wait()

    pending = []
    for app in range(2):
        for i in range(1, n_row):
            pltpu.make_async_remote_copy(
                src_ref=gathered.at[app, me_row], dst_ref=gathered.at[app, me_row],
                send_sem=gather_send.at[app], recv_sem=gather_recv.at[app],
                device_id=(row_peer(i), me_col), device_id_type=MESH).start()
        wait_others(gathered.at[app], gather_recv.at[app])
        for r in range(n_row):
            column[r * part_rows:(r + 1) * part_rows, :] = gathered[app, r]
        tile = column[pl.ds(first, 8), :]
        turned = pltpu.roll(tile, lax.rem(LANES - within, LANES), 1)
        cut = jnp.where(lane < LANES - within, turned, pltpu.roll(turned, 7, 0))
        cut_window[app] = cut
        windows, backs = [], []
        for h in range(hops):
            slot = app * hops + h
            copy = pltpu.make_async_remote_copy(
                src_ref=cut_window.at[app], dst_ref=far_window.at[slot],
                send_sem=window_send.at[slot], recv_sem=window_recv.at[slot],
                device_id=col_peer(-(h + 1)), device_id_type=MESH)
            copy.start()
            windows.append(copy)
        if app == 0:
            for load in loads:
                load.wait()
        projected = left_apply(mats[0], to_lanes(cut, chunks))
        seen = split_rows(projected)
        for h in range(hops):
            slot = app * hops + h
            back_out[slot] = lives[h] * to_tile(right_apply(seen, mats[h + 1]), chunks)
            copy = pltpu.make_async_remote_copy(
                src_ref=back_out.at[slot], dst_ref=back_in.at[slot],
                send_sem=back_send.at[slot], recv_sem=back_recv.at[slot],
                device_id=col_peer(h + 1), device_id_type=MESH)
            copy.start()
            backs.append(copy)
        inner = projected
        for h in range(hops):
            windows[h].wait_recv()
            inner = inner + lives[h] * left_apply(mats[h + 1], to_lanes(far_window[app * hops + h], chunks))
        total = to_tile(right_apply(split_rows(inner), mats[0]), chunks)
        for h in range(hops):
            backs[h].wait_recv()
            total = total + back_in[app * hops + h]
        turned = pltpu.roll(total, within, 1)
        placing[rows:rows + 8, :] = jnp.where(lane >= within, turned, pltpu.roll(turned, 1, 0))
        for t in range(n_row):
            outgoing[app, t] = placing[pl.ds(rows - first + t * part_rows, part_rows), :]
        for i in range(1, n_row):
            pltpu.make_async_remote_copy(
                src_ref=outgoing.at[app, row_peer(i)], dst_ref=incoming.at[app, me_row],
                send_sem=scatter_send.at[app], recv_sem=scatter_recv.at[app],
                device_id=(row_peer(i), me_col), device_id_type=MESH).start()
        incoming[app, me_row] = outgoing[app, me_row]
        wait_others(incoming.at[app], scatter_recv.at[app])
        summed = jnp.sum(incoming[app], axis=0)
        if app == 0:
            gathered[1, me_row] = summed
        else:
            out_ref[...] = summed
        pending += windows + backs
    for app in range(2):
        wait_others(gathered.at[app], gather_send.at[app])
        wait_others(outgoing.at[app], scatter_send.at[app])
    for copy in pending:
        copy.wait_send()


def on_device(sub_basis, coupling, pair_live, offsets, dual_in):
    n_row, n_col = lax.axis_size("row"), lax.axis_size("col")
    hops = coupling.shape[1]
    size = dual_in.shape[1]
    part_rows = size // LANES
    rows = n_row * part_rows
    depth, width = sub_basis.shape[1:]
    hbm = pl.BlockSpec(memory_space=pltpu.HBM)
    tiles = pltpu.VMEM((2 * hops, 8, LANES), jnp.float32)
    parts = pltpu.VMEM((2, n_row, part_rows, LANES), jnp.float32)
    dma = pltpu.SemaphoreType.DMA
    out = pl.pallas_call(
        lambda *refs: kernel(n_row, n_col, hops, *refs),
        out_shape=jax.ShapeDtypeStruct((part_rows, LANES), jnp.float32),
        in_specs=[hbm] * 5,
        out_specs=pl.BlockSpec(memory_space=pltpu.VMEM),
        scratch_shapes=[
            pltpu.VMEM((hops + 1, depth, width), jnp.bfloat16),
            parts,
            pltpu.VMEM((rows + 8, LANES), jnp.float32),
            pltpu.VMEM((2, 8, LANES), jnp.float32),
            tiles, tiles, tiles,
            pltpu.VMEM((2 * rows + 8, LANES), jnp.float32),
            parts, parts,
            pltpu.SMEM(pair_live.shape, jnp.int32),
            pltpu.SMEM(offsets.shape, jnp.int32),
            dma((hops + 1,)), dma((3,)), dma((2,)), dma((2,)),
            dma((2 * hops,)), dma((2 * hops,)), dma((2 * hops,)), dma((2 * hops,)),
            dma((2,)), dma((2,)),
        ],
        compiler_params=pltpu.CompilerParams(
            collective_id=0, has_side_effects=True, vmem_limit_bytes=60 * 1024 * 1024),
    )(sub_basis, coupling, pair_live, offsets, dual_in.reshape(part_rows, LANES))
    return out.reshape(1, size)


def solution(mesh):
    return jax.shard_map(
        on_device,
        mesh=mesh,
        in_specs=(
            P(("row", "col"), None, None),
            P(("row", "col"), None, None, None),
            P(("row", "col"), None),
            P(("row", "col")),
            P("col", "row"),
        ),
        out_specs=P("col", "row"),
        check_vma=False,
    )
```

```python
import jax
import jax.numpy as jnp
from jax import lax
from jax.experimental import pallas as pl
from jax.experimental.pallas import tpu as pltpu
from jax.sharding import PartitionSpec as P

LANES = 128
MESH = pl.DeviceIdType.MESH


def split_rows(vector):
    high = vector.astype(jnp.bfloat16).astype(jnp.float32)
    rest = vector - high
    middle = rest.astype(jnp.bfloat16).astype(jnp.float32)
    lowest = rest - middle
    row = lax.broadcasted_iota(jnp.int32, vector.shape, 0)
    picked = jnp.where(row == 0, high, jnp.where(row == 1, middle, lowest))
    return jnp.where(row < 3, picked, 0.0).astype(jnp.bfloat16)


def spread(products):
    return jnp.broadcast_to(jnp.sum(products, axis=0, keepdims=True), products.shape)


def left_apply(matrix, vector):
    return spread(lax.dot_general(
        split_rows(vector), matrix, (((1,), (1,)), ((), ())),
        preferred_element_type=jnp.float32,
    ))


def right_apply(rows, matrix):
    return spread(jnp.dot(rows, matrix, preferred_element_type=jnp.float32))


def to_lanes(tile, chunks):
    return jnp.concatenate(
        [jnp.broadcast_to(tile[j:j + 1, :], (8, LANES)) for j in range(chunks)], axis=1)


def to_tile(vector, chunks):
    row = lax.broadcasted_iota(jnp.int32, (8, LANES), 0)
    tile = jnp.zeros((8, LANES), jnp.float32)
    for j in range(chunks):
        tile = jnp.where(row == j, vector[:, j * LANES:(j + 1) * LANES], tile)
    return tile


def kernel(n_row, n_col, hops, basis_hbm, coupling_hbm, live_hbm, offset_hbm, dual_hbm, out_ref,
           mats, gathered, column, middle, row_offsets, cut_window, far_window, back_out, back_in, placing, outgoing, incoming,
           live_ref, offset_ref, load_sems, small_sems, gather_send, gather_recv,
           middle_send, middle_recv, offset_send, offset_recv, window_send, window_recv, back_send, back_recv, scatter_send, scatter_recv):
    me_row, me_col = lax.axis_index("row"), lax.axis_index("col")
    part_rows = dual_hbm.shape[0]
    rows = n_row * part_rows
    chunks = mats.shape[2] // LANES
    others = n_row - 1

    small = [
        pltpu.make_async_copy(dual_hbm, gathered.at[me_row], small_sems.at[0]),
        pltpu.make_async_copy(offset_hbm, offset_ref, small_sems.at[1]),
        pltpu.make_async_copy(live_hbm, live_ref, small_sems.at[2]),
    ]
    loads = [pltpu.make_async_copy(basis_hbm.at[0], mats.at[0], load_sems.at[0])]
    for h in range(hops):
        loads.append(pltpu.make_async_copy(coupling_hbm.at[0, h], mats.at[h + 1], load_sems.at[h + 1]))
    for copy in small + loads:
        copy.start()

    barrier = pltpu.get_barrier_semaphore()
    for i in range(1, n_row):
        pl.semaphore_signal(barrier, inc=1, device_id=(lax.rem(me_row + i, n_row), me_col), device_id_type=MESH)
    shifts = sorted({d % n_col for d in range(-hops, hops + 1)} - {0})
    for shift in shifts:
        pl.semaphore_signal(barrier, inc=1, device_id=(me_row, lax.rem(me_col + shift, n_col)), device_id_type=MESH)

    column[rows:, :] = jnp.zeros((column.shape[0] - rows, LANES), jnp.float32)
    placing[...] = jnp.zeros(placing.shape, jnp.float32)
    middle[:, :8, :] = jnp.zeros((n_row, 8, LANES), jnp.float32)
    middle[:, 16:, :] = jnp.zeros((n_row, 8, LANES), jnp.float32)
    for copy in small:
        copy.wait()
    start = offset_ref[0]
    first = start // LANES
    within = start - first * LANES
    lives = [live_ref[0, h].astype(jnp.float32) for h in range(hops)]
    lane = lax.broadcasted_iota(jnp.int32, (8, LANES), 1)
    pl.semaphore_wait(barrier, others + len(shifts))

    def wait_tiles(sem):
        tiles = middle.at[pl.ds(0, others), pl.ds(8, 8)]
        pltpu.make_async_copy(tiles, tiles, sem).wait()

    def row_peer(i):
        return lax.rem(me_row + i, n_row)

    def col_peer(shift):
        return (me_row, lax.rem(me_col + (shift % n_col), n_col))

    def wait_others(ref, sem):
        pltpu.make_async_copy(ref.at[pl.ds(0, others)], ref.at[pl.ds(0, others)], sem).wait()

    def cut_at(tile):
        turned = pltpu.roll(tile, lax.rem(LANES - within, LANES), 1)
        return jnp.where(lane < LANES - within, turned, pltpu.roll(turned, 7, 0))

    for i in range(1, n_row):
        pltpu.make_async_remote_copy(
            src_ref=gathered.at[me_row], dst_ref=gathered.at[me_row],
            send_sem=gather_send.at[0], recv_sem=gather_recv.at[0],
            device_id=(row_peer(i), me_col), device_id_type=MESH).start()
    for i in range(1, n_row):
        pltpu.make_async_remote_copy(
            src_ref=offset_ref, dst_ref=row_offsets.at[me_row],
            send_sem=offset_send.at[0], recv_sem=offset_recv.at[0],
            device_id=(row_peer(i), me_col), device_id_type=MESH).start()
    wait_others(gathered, gather_recv.at[0])
    for r in range(n_row):
        column[r * part_rows:(r + 1) * part_rows, :] = gathered[r]
    cut = cut_at(column[pl.ds(first, 8), :])

    pending = []
    for app in range(2):
        cut_window[app] = cut
        windows, backs = [], []
        for h in range(hops):
            slot = app * hops + h
            copy = pltpu.make_async_remote_copy(
                src_ref=cut_window.at[app], dst_ref=far_window.at[slot],
                send_sem=window_send.at[slot], recv_sem=window_recv.at[slot],
                device_id=col_peer(-(h + 1)), device_id_type=MESH)
            copy.start()
            windows.append(copy)
        if app == 0:
            for load in loads:
                load.wait()
        projected = left_apply(mats[0], to_lanes(cut, chunks))
        seen = split_rows(projected)
        for h in range(hops):
            slot = app * hops + h
            back_out[slot] = lives[h] * to_tile(right_apply(seen, mats[h + 1]), chunks)
            copy = pltpu.make_async_remote_copy(
                src_ref=back_out.at[slot], dst_ref=back_in.at[slot],
                send_sem=back_send.at[slot], recv_sem=back_recv.at[slot],
                device_id=col_peer(h + 1), device_id_type=MESH)
            copy.start()
            backs.append(copy)
        inner = projected
        for h in range(hops):
            windows[h].wait_recv()
            inner = inner + lives[h] * left_apply(mats[h + 1], to_lanes(far_window[app * hops + h], chunks))
        total = to_tile(right_apply(split_rows(inner), mats[0]), chunks)
        for h in range(hops):
            backs[h].wait_recv()
            total = total + back_in[app * hops + h]
        turned = pltpu.roll(total, within, 1)
        total = jnp.where(lane >= within, turned, pltpu.roll(turned, 1, 0))
        pending += windows + backs
        if app == 0:
            middle[me_row, 8:16, :] = total
            for i in range(1, n_row):
                pltpu.make_async_remote_copy(
                    src_ref=middle.at[me_row, pl.ds(8, 8)], dst_ref=middle.at[me_row, pl.ds(8, 8)],
                    send_sem=middle_send.at[0], recv_sem=middle_recv.at[0],
                    device_id=(row_peer(i), me_col), device_id_type=MESH).start()
            wait_others(row_offsets, offset_recv.at[0])
            shifts = [jnp.clip(first - row_offsets[lax.rem(me_row + i, n_row), 0] // LANES, -8, 8) for i in range(1, n_row)]
            wait_tiles(middle_recv.at[0])
            tile = total
            for i in range(1, n_row):
                tile = tile + middle[lax.rem(me_row + i, n_row), pl.ds(8 + shifts[i - 1], 8), :]
            cut = cut_at(tile)
    placing[rows:rows + 8, :] = total
    for t in range(n_row):
        outgoing[t] = placing[pl.ds(rows - first + t * part_rows, part_rows), :]
    for i in range(1, n_row):
        pltpu.make_async_remote_copy(
            src_ref=outgoing.at[row_peer(i)], dst_ref=incoming.at[me_row],
            send_sem=scatter_send.at[0], recv_sem=scatter_recv.at[0],
            device_id=(row_peer(i), me_col), device_id_type=MESH).start()
    incoming[me_row] = outgoing[me_row]
    wait_others(incoming, scatter_recv.at[0])
    out_ref[...] = jnp.sum(incoming[...], axis=0)
    wait_others(gathered, gather_send.at[0])
    wait_others(row_offsets, offset_send.at[0])
    wait_tiles(middle_send.at[0])
    wait_others(outgoing, scatter_send.at[0])
    for copy in pending:
        copy.wait_send()


def on_device(sub_basis, coupling, pair_live, offsets, dual_in):
    n_row, n_col = lax.axis_size("row"), lax.axis_size("col")
    hops = coupling.shape[1]
    size = dual_in.shape[1]
    part_rows = size // LANES
    rows = n_row * part_rows
    depth, width = sub_basis.shape[1:]
    hbm = pl.BlockSpec(memory_space=pltpu.HBM)
    tiles = pltpu.VMEM((2 * hops, 8, LANES), jnp.float32)
    parts = pltpu.VMEM((n_row, part_rows, LANES), jnp.float32)
    dma = pltpu.SemaphoreType.DMA
    out = pl.pallas_call(
        lambda *refs: kernel(n_row, n_col, hops, *refs),
        out_shape=pltpu.VMEM((part_rows, LANES), jnp.float32),
        in_specs=[hbm] * 5,
        out_specs=pl.BlockSpec(memory_space=pltpu.VMEM),
        scratch_shapes=[
            pltpu.VMEM((hops + 1, depth, width), jnp.bfloat16),
            parts,
            pltpu.VMEM((rows + 8, LANES), jnp.float32),
            pltpu.VMEM((n_row, 24, LANES), jnp.float32),
            pltpu.SMEM((n_row, 1), jnp.int32),
            pltpu.VMEM((2, 8, LANES), jnp.float32),
            tiles, tiles, tiles,
            pltpu.VMEM((2 * rows + 8, LANES), jnp.float32),
            parts, parts,
            pltpu.SMEM(pair_live.shape, jnp.int32),
            pltpu.SMEM(offsets.shape, jnp.int32),
            dma((hops + 1,)), dma((3,)), dma((1,)), dma((1,)),
            dma((1,)), dma((1,)), dma((1,)), dma((1,)),
            dma((2 * hops,)), dma((2 * hops,)), dma((2 * hops,)), dma((2 * hops,)),
            dma((1,)), dma((1,)),
        ],
        compiler_params=pltpu.CompilerParams(
            collective_id=0, has_side_effects=True, vmem_limit_bytes=60 * 1024 * 1024),
    )(sub_basis, coupling, pair_live, offsets, dual_in.reshape(part_rows, LANES))
    return out.reshape(1, size)


def solution(mesh):
    return jax.shard_map(
        on_device,
        mesh=mesh,
        in_specs=(
            P(("row", "col"), None, None),
            P(("row", "col"), None, None, None),
            P(("row", "col"), None),
            P(("row", "col")),
            P("col", "row"),
        ),
        out_specs=P("col", "row"),
        check_vma=False,
    )
```

```python
import jax
import jax.numpy as jnp
from jax import lax
from jax.experimental import pallas as pl
from jax.experimental.pallas import tpu as pltpu
from jax.sharding import PartitionSpec as P

LANES = 128
MESH = pl.DeviceIdType.MESH


def split_rows(vector):
    high = vector.astype(jnp.bfloat16).astype(jnp.float32)
    rest = vector - high
    middle = rest.astype(jnp.bfloat16).astype(jnp.float32)
    lowest = rest - middle
    row = lax.broadcasted_iota(jnp.int32, vector.shape, 0)
    picked = jnp.where(row == 0, high, jnp.where(row == 1, middle, lowest))
    return jnp.where(row < 3, picked, 0.0).astype(jnp.bfloat16)


def spread(products):
    return jnp.broadcast_to(jnp.sum(products, axis=0, keepdims=True), products.shape)


def left_apply(matrix, vector):
    return spread(lax.dot_general(
        split_rows(vector), matrix, (((1,), (1,)), ((), ())),
        preferred_element_type=jnp.float32,
    ))


def right_apply(rows, matrix):
    return spread(jnp.dot(rows, matrix, preferred_element_type=jnp.float32))


def to_lanes(tile, chunks):
    return jnp.concatenate(
        [jnp.broadcast_to(tile[j:j + 1, :], (8, LANES)) for j in range(chunks)], axis=1)


def to_tile(vector, chunks):
    row = lax.broadcasted_iota(jnp.int32, (8, LANES), 0)
    tile = jnp.zeros((8, LANES), jnp.float32)
    for j in range(chunks):
        tile = jnp.where(row == j, vector[:, j * LANES:(j + 1) * LANES], tile)
    return tile


def kernel(n_row, n_col, hops, basis_hbm, coupling_hbm, live_hbm, offset_hbm, dual_hbm, out_ref,
           mats, turned_basis, blocks, gathered, column, middle, row_offsets, cut_window, far_window, back_out, back_in, placing, outgoing, incoming,
           live_ref, offset_ref, load_sems, small_sems, gather_send, gather_recv,
           middle_send, middle_recv, offset_send, offset_recv, window_send, window_recv, back_send, back_recv, scatter_send, scatter_recv):
    me_row, me_col = lax.axis_index("row"), lax.axis_index("col")
    part_rows = dual_hbm.shape[0]
    rows = n_row * part_rows
    chunks = mats.shape[2] // LANES
    others = n_row - 1

    small = [
        pltpu.make_async_copy(dual_hbm, gathered.at[me_row], small_sems.at[0]),
        pltpu.make_async_copy(offset_hbm, offset_ref, small_sems.at[1]),
        pltpu.make_async_copy(live_hbm, live_ref, small_sems.at[2]),
    ]
    loads = [pltpu.make_async_copy(basis_hbm.at[0], mats.at[0], load_sems.at[0])]
    for h in range(hops):
        loads.append(pltpu.make_async_copy(coupling_hbm.at[0, h], mats.at[h + 1], load_sems.at[h + 1]))
    for copy in small:
        copy.start()

    barrier = pltpu.get_barrier_semaphore()
    for i in range(1, n_row):
        pl.semaphore_signal(barrier, inc=1, device_id=(lax.rem(me_row + i, n_row), me_col), device_id_type=MESH)
    shifts = sorted({d % n_col for d in range(-hops, hops + 1)} - {0})
    for shift in shifts:
        pl.semaphore_signal(barrier, inc=1, device_id=(me_row, lax.rem(me_col + shift, n_col)), device_id_type=MESH)

    for load in loads:
        load.start()
    column[rows:, :] = jnp.zeros((column.shape[0] - rows, LANES), jnp.float32)
    placing[...] = jnp.zeros(placing.shape, jnp.float32)
    middle[:, :8, :] = jnp.zeros((n_row, 8, LANES), jnp.float32)
    middle[:, 16:, :] = jnp.zeros((n_row, 8, LANES), jnp.float32)
    for copy in small:
        copy.wait()
    start = offset_ref[0]
    first = start // LANES
    within = start - first * LANES
    lives = [live_ref[0, h].astype(jnp.float32) for h in range(hops)]
    lane = lax.broadcasted_iota(jnp.int32, (8, LANES), 1)
    pl.semaphore_wait(barrier, others + len(shifts))

    def wait_tiles(sem):
        tiles = middle.at[pl.ds(0, others), pl.ds(8, 8)]
        pltpu.make_async_copy(tiles, tiles, sem).wait()

    def row_peer(i):
        return lax.rem(me_row + i, n_row)

    def col_peer(shift):
        return (me_row, lax.rem(me_col + (shift % n_col), n_col))

    def wait_others(ref, sem):
        pltpu.make_async_copy(ref.at[pl.ds(0, others)], ref.at[pl.ds(0, others)], sem).wait()

    def cut_at(tile):
        turned = pltpu.roll(tile, lax.rem(LANES - within, LANES), 1)
        return jnp.where(lane < LANES - within, turned, pltpu.roll(turned, 7, 0))

    for i in range(1, n_row):
        pltpu.make_async_remote_copy(
            src_ref=gathered.at[me_row], dst_ref=gathered.at[me_row],
            send_sem=gather_send.at[0], recv_sem=gather_recv.at[0],
            device_id=(row_peer(i), me_col), device_id_type=MESH).start()
    for i in range(1, n_row):
        pltpu.make_async_remote_copy(
            src_ref=offset_ref, dst_ref=row_offsets.at[me_row],
            send_sem=offset_send.at[0], recv_sem=offset_recv.at[0],
            device_id=(row_peer(i), me_col), device_id_type=MESH).start()
    for load in loads:
        load.wait()
    turned_basis[...] = mats[0].T
    step = min(256, blocks.shape[2])
    for h in range(hops):
        for n in range(0, blocks.shape[2], step):
            blocks[h, :, n:n + step] = jnp.dot(
                turned_basis[...], mats[h + 1, :, n:n + step],
                preferred_element_type=jnp.float32).astype(jnp.bfloat16)
    wait_others(gathered, gather_recv.at[0])
    for r in range(n_row):
        column[r * part_rows:(r + 1) * part_rows, :] = gathered[r]
    cut = cut_at(column[pl.ds(first, 8), :])

    pending = []
    for app in range(2):
        cut_window[app] = cut
        windows, backs = [], []
        for h in range(hops):
            slot = app * hops + h
            copy = pltpu.make_async_remote_copy(
                src_ref=cut_window.at[app], dst_ref=far_window.at[slot],
                send_sem=window_send.at[slot], recv_sem=window_recv.at[slot],
                device_id=col_peer(-(h + 1)), device_id_type=MESH)
            copy.start()
            windows.append(copy)
        seen = split_rows(to_lanes(cut, chunks))
        for h in range(hops):
            slot = app * hops + h
            back_out[slot] = lives[h] * to_tile(right_apply(seen, blocks[h]), chunks)
            copy = pltpu.make_async_remote_copy(
                src_ref=back_out.at[slot], dst_ref=back_in.at[slot],
                send_sem=back_send.at[slot], recv_sem=back_recv.at[slot],
                device_id=col_peer(h + 1), device_id_type=MESH)
            copy.start()
            backs.append(copy)
        projected = right_apply(seen, turned_basis[...])
        vector = right_apply(split_rows(projected), mats[0])
        for h in range(hops):
            windows[h].wait_recv()
        for h in range(hops):
            vector = vector + lives[h] * left_apply(blocks[h], to_lanes(far_window[app * hops + h], chunks))
        total = to_tile(vector, chunks)
        for h in range(hops):
            backs[h].wait_recv()
            total = total + back_in[app * hops + h]
        turned = pltpu.roll(total, within, 1)
        total = jnp.where(lane >= within, turned, pltpu.roll(turned, 1, 0))
        pending += windows + backs
        if app == 0:
            middle[me_row, 8:16, :] = total
            for i in range(1, n_row):
                pltpu.make_async_remote_copy(
                    src_ref=middle.at[me_row, pl.ds(8, 8)], dst_ref=middle.at[me_row, pl.ds(8, 8)],
                    send_sem=middle_send.at[0], recv_sem=middle_recv.at[0],
                    device_id=(row_peer(i), me_col), device_id_type=MESH).start()
            wait_others(row_offsets, offset_recv.at[0])
            shifts = [jnp.clip(first - row_offsets[lax.rem(me_row + i, n_row), 0] // LANES, -8, 8) for i in range(1, n_row)]
            wait_tiles(middle_recv.at[0])
            tile = total
            for i in range(1, n_row):
                tile = tile + middle[lax.rem(me_row + i, n_row), pl.ds(8 + shifts[i - 1], 8), :]
            cut = cut_at(tile)
    placing[rows:rows + 8, :] = total
    for t in range(n_row):
        outgoing[t] = placing[pl.ds(rows - first + t * part_rows, part_rows), :]
    for i in range(1, n_row):
        pltpu.make_async_remote_copy(
            src_ref=outgoing.at[row_peer(i)], dst_ref=incoming.at[me_row],
            send_sem=scatter_send.at[0], recv_sem=scatter_recv.at[0],
            device_id=(row_peer(i), me_col), device_id_type=MESH).start()
    incoming[me_row] = outgoing[me_row]
    wait_others(incoming, scatter_recv.at[0])
    out_ref[...] = jnp.sum(incoming[...], axis=0)
    wait_others(gathered, gather_send.at[0])
    wait_others(row_offsets, offset_send.at[0])
    wait_tiles(middle_send.at[0])
    wait_others(outgoing, scatter_send.at[0])
    for copy in pending:
        copy.wait_send()


def on_device(sub_basis, coupling, pair_live, offsets, dual_in):
    n_row, n_col = lax.axis_size("row"), lax.axis_size("col")
    hops = coupling.shape[1]
    size = dual_in.shape[1]
    part_rows = size // LANES
    rows = n_row * part_rows
    depth, width = sub_basis.shape[1:]
    hbm = pl.BlockSpec(memory_space=pltpu.HBM)
    tiles = pltpu.VMEM((2 * hops, 8, LANES), jnp.float32)
    parts = pltpu.VMEM((n_row, part_rows, LANES), jnp.float32)
    dma = pltpu.SemaphoreType.DMA
    out = pl.pallas_call(
        lambda *refs: kernel(n_row, n_col, hops, *refs),
        out_shape=pltpu.VMEM((part_rows, LANES), jnp.float32),
        in_specs=[hbm] * 5,
        out_specs=pl.BlockSpec(memory_space=pltpu.VMEM),
        scratch_shapes=[
            pltpu.VMEM((hops + 1, depth, width), jnp.bfloat16),
            pltpu.VMEM((width, depth), jnp.bfloat16),
            pltpu.VMEM((hops, width, width), jnp.bfloat16),
            parts,
            pltpu.VMEM((rows + 8, LANES), jnp.float32),
            pltpu.VMEM((n_row, 24, LANES), jnp.float32),
            pltpu.SMEM((n_row, 1), jnp.int32),
            pltpu.VMEM((2, 8, LANES), jnp.float32),
            tiles, tiles, tiles,
            pltpu.VMEM((2 * rows + 8, LANES), jnp.float32),
            parts, parts,
            pltpu.SMEM(pair_live.shape, jnp.int32),
            pltpu.SMEM(offsets.shape, jnp.int32),
            dma((hops + 1,)), dma((3,)), dma((1,)), dma((1,)),
            dma((1,)), dma((1,)), dma((1,)), dma((1,)),
            dma((2 * hops,)), dma((2 * hops,)), dma((2 * hops,)), dma((2 * hops,)),
            dma((1,)), dma((1,)),
        ],
        compiler_params=pltpu.CompilerParams(
            collective_id=0, has_side_effects=True, vmem_limit_bytes=60 * 1024 * 1024),
    )(sub_basis, coupling, pair_live, offsets, dual_in.reshape(part_rows, LANES))
    return out.reshape(1, size)


def solution(mesh):
    return jax.shard_map(
        on_device,
        mesh=mesh,
        in_specs=(
            P(("row", "col"), None, None),
            P(("row", "col"), None, None, None),
            P(("row", "col"), None),
            P(("row", "col")),
            P("col", "row"),
        ),
        out_specs=P("col", "row"),
        check_vma=False,
    )
```

```python
import jax
import jax.numpy as jnp
from jax import lax
from jax.experimental import pallas as pl
from jax.experimental.pallas import tpu as pltpu
from jax.sharding import PartitionSpec as P

LANES = 128
MESH = pl.DeviceIdType.MESH


def split_rows(vector):
    high = vector.astype(jnp.bfloat16).astype(jnp.float32)
    rest = vector - high
    middle = rest.astype(jnp.bfloat16).astype(jnp.float32)
    lowest = rest - middle
    row = lax.broadcasted_iota(jnp.int32, vector.shape, 0)
    picked = jnp.where(row == 0, high, jnp.where(row == 1, middle, lowest))
    return jnp.where(row < 3, picked, 0.0).astype(jnp.bfloat16)


def spread(products):
    return jnp.broadcast_to(jnp.sum(products, axis=0, keepdims=True), products.shape)


def left_products(matrix, vector):
    return lax.dot_general(
        split_rows(vector), matrix, (((1,), (1,)), ((), ())),
        preferred_element_type=jnp.float32,
    )


def right_apply(rows, matrix):
    return spread(jnp.dot(rows, matrix, preferred_element_type=jnp.float32))


def to_lanes(tile, chunks):
    return jnp.concatenate(
        [jnp.broadcast_to(tile[j:j + 1, :], (8, LANES)) for j in range(chunks)], axis=1)


def to_tile(vector, chunks):
    row = lax.broadcasted_iota(jnp.int32, (8, LANES), 0)
    tile = jnp.zeros((8, LANES), jnp.float32)
    for j in range(chunks):
        tile = jnp.where(row == j, vector[:, j * LANES:(j + 1) * LANES], tile)
    return tile


def kernel(n_row, n_col, hops, basis_hbm, coupling_hbm, live_hbm, offset_hbm, dual_hbm, out_ref,
           mats, turned_basis, blocks, gathered, column, middle, row_offsets, cut_window, far_window, back_out, back_in, placing, outgoing, incoming,
           live_ref, offset_ref, load_sems, small_sems, gather_send, gather_recv,
           middle_send, middle_recv, offset_send, offset_recv, window_send, window_recv, back_send, back_recv, scatter_send, scatter_recv):
    me_row, me_col = lax.axis_index("row"), lax.axis_index("col")
    part_rows = dual_hbm.shape[0]
    rows = n_row * part_rows
    chunks = mats.shape[2] // LANES
    others = n_row - 1

    small = [
        pltpu.make_async_copy(dual_hbm, gathered.at[me_row], small_sems.at[0]),
        pltpu.make_async_copy(offset_hbm, offset_ref, small_sems.at[1]),
        pltpu.make_async_copy(live_hbm, live_ref, small_sems.at[2]),
    ]
    loads = [pltpu.make_async_copy(basis_hbm.at[0], mats.at[0], load_sems.at[0])]
    for h in range(hops):
        loads.append(pltpu.make_async_copy(coupling_hbm.at[0, h], mats.at[h + 1], load_sems.at[h + 1]))
    for copy in small:
        copy.start()

    barrier = pltpu.get_barrier_semaphore()
    for i in range(1, n_row):
        pl.semaphore_signal(barrier, inc=1, device_id=(lax.rem(me_row + i, n_row), me_col), device_id_type=MESH)
    shifts = sorted({d % n_col for d in range(-hops, hops + 1)} - {0})
    for shift in shifts:
        pl.semaphore_signal(barrier, inc=1, device_id=(me_row, lax.rem(me_col + shift, n_col)), device_id_type=MESH)

    for load in loads:
        load.start()
    for copy in small:
        copy.wait()
    start = offset_ref[0]
    first = start // LANES
    within = start - first * LANES
    lives = [live_ref[0, h].astype(jnp.float32) for h in range(hops)]
    lane = lax.broadcasted_iota(jnp.int32, (8, LANES), 1)
    pl.semaphore_wait(barrier, others + len(shifts))

    def wait_tiles(sem):
        tiles = middle.at[pl.ds(0, others), pl.ds(8, 8)]
        pltpu.make_async_copy(tiles, tiles, sem).wait()

    def row_peer(i):
        return lax.rem(me_row + i, n_row)

    def col_peer(shift):
        return (me_row, lax.rem(me_col + (shift % n_col), n_col))

    def wait_others(ref, sem):
        pltpu.make_async_copy(ref.at[pl.ds(0, others)], ref.at[pl.ds(0, others)], sem).wait()

    def cut_at(tile):
        turned = pltpu.roll(tile, lax.rem(LANES - within, LANES), 1)
        return jnp.where(lane < LANES - within, turned, pltpu.roll(turned, 7, 0))

    for i in range(1, n_row):
        pltpu.make_async_remote_copy(
            src_ref=gathered.at[me_row], dst_ref=gathered.at[me_row],
            send_sem=gather_send.at[0], recv_sem=gather_recv.at[0],
            device_id=(row_peer(i), me_col), device_id_type=MESH).start()
    column[rows:, :] = jnp.zeros((column.shape[0] - rows, LANES), jnp.float32)
    placing[...] = jnp.zeros(placing.shape, jnp.float32)
    middle[:, :8, :] = jnp.zeros((n_row, 8, LANES), jnp.float32)
    middle[:, 16:, :] = jnp.zeros((n_row, 8, LANES), jnp.float32)
    for i in range(1, n_row):
        pltpu.make_async_remote_copy(
            src_ref=offset_ref, dst_ref=row_offsets.at[me_row],
            send_sem=offset_send.at[0], recv_sem=offset_recv.at[0],
            device_id=(row_peer(i), me_col), device_id_type=MESH).start()
    for load in loads:
        load.wait()
    turned_basis[...] = mats[0].T
    step = min(256, blocks.shape[2])
    for h in range(hops):
        for n in range(0, blocks.shape[2], step):
            blocks[h, :, n:n + step] = jnp.dot(
                turned_basis[...], mats[h + 1, :, n:n + step],
                preferred_element_type=jnp.float32).astype(jnp.bfloat16)
    wait_others(gathered, gather_recv.at[0])
    for r in range(n_row):
        column[r * part_rows:(r + 1) * part_rows, :] = gathered[r]
    cut = cut_at(column[pl.ds(first, 8), :])

    pending = []
    for app in range(2):
        cut_window[app] = cut
        windows, backs = [], []
        for h in range(hops):
            slot = app * hops + h
            copy = pltpu.make_async_remote_copy(
                src_ref=cut_window.at[app], dst_ref=far_window.at[slot],
                send_sem=window_send.at[slot], recv_sem=window_recv.at[slot],
                device_id=col_peer(-(h + 1)), device_id_type=MESH)
            copy.start()
            windows.append(copy)
        seen = split_rows(to_lanes(cut, chunks))
        for h in range(hops):
            slot = app * hops + h
            back_out[slot] = lives[h] * to_tile(right_apply(seen, blocks[h]), chunks)
            copy = pltpu.make_async_remote_copy(
                src_ref=back_out.at[slot], dst_ref=back_in.at[slot],
                send_sem=back_send.at[slot], recv_sem=back_recv.at[slot],
                device_id=col_peer(h + 1), device_id_type=MESH)
            copy.start()
            backs.append(copy)
        projected = right_apply(seen, turned_basis[...])
        vector = right_apply(split_rows(projected), mats[0])
        for h in range(hops):
            windows[h].wait_recv()
        ahead = [lives[h] * left_products(blocks[h], to_lanes(far_window[app * hops + h], chunks)) for h in range(hops)]
        vector = vector + spread(sum(ahead))
        total = to_tile(vector, chunks)
        for h in range(hops):
            backs[h].wait_recv()
            total = total + back_in[app * hops + h]
        turned = pltpu.roll(total, within, 1)
        total = jnp.where(lane >= within, turned, pltpu.roll(turned, 1, 0))
        pending += windows + backs
        if app == 0:
            middle[me_row, 8:16, :] = total
            for i in range(1, n_row):
                pltpu.make_async_remote_copy(
                    src_ref=middle.at[me_row, pl.ds(8, 8)], dst_ref=middle.at[me_row, pl.ds(8, 8)],
                    send_sem=middle_send.at[0], recv_sem=middle_recv.at[0],
                    device_id=(row_peer(i), me_col), device_id_type=MESH).start()
            wait_others(row_offsets, offset_recv.at[0])
            shifts = [jnp.clip(first - row_offsets[lax.rem(me_row + i, n_row), 0] // LANES, -8, 8) for i in range(1, n_row)]
            wait_tiles(middle_recv.at[0])
            tile = total
            for i in range(1, n_row):
                tile = tile + middle[lax.rem(me_row + i, n_row), pl.ds(8 + shifts[i - 1], 8), :]
            cut = cut_at(tile)
    placing[rows:rows + 8, :] = total
    for i in list(range(1, n_row)) + [0]:
        peer = row_peer(i)
        outgoing[peer] = placing[pl.ds(rows - first + peer * part_rows, part_rows), :]
        if i > 0:
            pltpu.make_async_remote_copy(
                src_ref=outgoing.at[peer], dst_ref=incoming.at[me_row],
                send_sem=scatter_send.at[0], recv_sem=scatter_recv.at[0],
                device_id=(peer, me_col), device_id_type=MESH).start()
    incoming[me_row] = outgoing[me_row]
    wait_others(incoming, scatter_recv.at[0])
    out_ref[...] = jnp.sum(incoming[...], axis=0)
    wait_others(gathered, gather_send.at[0])
    wait_others(row_offsets, offset_send.at[0])
    wait_tiles(middle_send.at[0])
    wait_others(outgoing, scatter_send.at[0])
    for copy in pending:
        copy.wait_send()


def on_device(sub_basis, coupling, pair_live, offsets, dual_in):
    n_row, n_col = lax.axis_size("row"), lax.axis_size("col")
    hops = coupling.shape[1]
    size = dual_in.shape[1]
    part_rows = size // LANES
    rows = n_row * part_rows
    depth, width = sub_basis.shape[1:]
    hbm = pl.BlockSpec(memory_space=pltpu.HBM)
    tiles = pltpu.VMEM((2 * hops, 8, LANES), jnp.float32)
    parts = pltpu.VMEM((n_row, part_rows, LANES), jnp.float32)
    dma = pltpu.SemaphoreType.DMA
    out = pl.pallas_call(
        lambda *refs: kernel(n_row, n_col, hops, *refs),
        out_shape=pltpu.VMEM((part_rows, LANES), jnp.float32),
        in_specs=[hbm] * 5,
        out_specs=pl.BlockSpec(memory_space=pltpu.VMEM),
        scratch_shapes=[
            pltpu.VMEM((hops + 1, depth, width), jnp.bfloat16),
            pltpu.VMEM((width, depth), jnp.bfloat16),
            pltpu.VMEM((hops, width, width), jnp.bfloat16),
            parts,
            pltpu.VMEM((rows + 8, LANES), jnp.float32),
            pltpu.VMEM((n_row, 24, LANES), jnp.float32),
            pltpu.SMEM((n_row, 1), jnp.int32),
            pltpu.VMEM((2, 8, LANES), jnp.float32),
            tiles, tiles, tiles,
            pltpu.VMEM((2 * rows + 8, LANES), jnp.float32),
            parts, parts,
            pltpu.SMEM(pair_live.shape, jnp.int32),
            pltpu.SMEM(offsets.shape, jnp.int32),
            dma((hops + 1,)), dma((3,)), dma((1,)), dma((1,)),
            dma((1,)), dma((1,)), dma((1,)), dma((1,)),
            dma((2 * hops,)), dma((2 * hops,)), dma((2 * hops,)), dma((2 * hops,)),
            dma((1,)), dma((1,)),
        ],
        compiler_params=pltpu.CompilerParams(
            collective_id=0, has_side_effects=True, vmem_limit_bytes=60 * 1024 * 1024),
    )(sub_basis, coupling, pair_live, offsets, dual_in.reshape(part_rows, LANES))
    return out.reshape(1, size)


def solution(mesh):
    return jax.shard_map(
        on_device,
        mesh=mesh,
        in_specs=(
            P(("row", "col"), None, None),
            P(("row", "col"), None, None, None),
            P(("row", "col"), None),
            P(("row", "col")),
            P("col", "row"),
        ),
        out_specs=P("col", "row"),
        check_vma=False,
    )
```
